32 devices in a mesh: expert: 8 (over z, core), shard: 4 (over y, x).
Axes of the slice: x: 2, y: 2, z: 4, core: 2. Of those that a mesh axis runs over, the one named last changes fastest.
Arguments:
- hidden_in: bfloat16 [32, 256, 1024], P(('expert', 'shard')), may hold values from -6 to 6
- segment_ids: int32 [32, 256], P(('expert', 'shard')), may hold values from 0 to 3, never falling along the last dimension, each value on 1 to 128 neighbouring positions
- pad_mask: int32 [32, 256], P(('expert', 'shard')), may hold values from 0 to 1, as said below
- expert_choice: int32 [32, 256, 8], P(('expert', 'shard')), may hold values from 0 to 31, all different within a row
- slot_rank: int32 [32, 256], P(('expert', 'shard')), may hold values from 0 to 255, each once within a row
- attn_gain: bfloat16 [1024], P('shard'), may hold values from 0.5 to 1.5
- query_weight: bfloat16 [1024, 1024], P('shard'), may hold values from -0.1875 to 0.1875
- key_weight: bfloat16 [1024, 512], P('shard'), may hold values from -0.1875 to 0.1875
- value_weight: bfloat16 [1024, 512], P('shard'), may hold values from -0.1875 to 0.1875
- output_weight: bfloat16 [1024, 1024], P('shard'), may hold values from -1 to 1
- moe_gain: bfloat16 [1024], P('shard'), may hold values from 0.5 to 1.5
- router_weight: bfloat16 [1024, 32], P('shard'), may hold values from -0.25 to 0.25
- gate_weight: bfloat16 [32, 1024, 512], P('expert'), may hold values from -0.1875 to 0.1875
- up_weight: bfloat16 [32, 1024, 512], P('expert'), may hold values from -0.1875 to 0.1875
- down_weight: bfloat16 [32, 512, 1024], P('expert'), may hold values from -1 to 1
- out_grad: bfloat16 [32, 256, 1024], P(('expert', 'shard')), may hold values from -6 to 6
Outputs:
- block_out: bfloat16 [32, 256, 1024], P(('expert', 'shard'))
- in_grad: bfloat16 [32, 256, 1024], P(('expert', 'shard'))
- attn_gain_grad: float32 [1024], P('shard')
- query_weight_grad: float32 [1024, 1024], P('shard')
- key_weight_grad: float32 [1024, 512], P('shard')
- value_weight_grad: float32 [1024, 512], P('shard')
- output_weight_grad: float32 [1024, 1024], P('shard')
- moe_gain_grad: float32 [1024], P('shard')
- router_weight_grad: float32 [1024, 32], P('shard')
- gate_weight_grad: float32 [32, 1024, 512], P('expert')
- up_weight_grad: float32 [32, 1024, 512], P('expert')
- down_weight_grad: float32 [32, 512, 1024], P('expert')
The draws below stay inside these ranges and needn't reach their ends.
Inputs may be any that keep to these rules, and one draw needn't show every extreme that they name: `segment_ids`: along each sequence the document numbers never fall; each document holds at most 128 tokens and one holds exactly that many. `pad_mask`: each sequence's live tokens (1) come first; its padded tail (0) holds at most 64 tokens, and some sequence has exactly that many. `expert_choice`: the 8 experts of a token are different. `slot_rank`: each sequence holds every number of 0 to 255 once.
All inputs are finite; a program needn't handle non-finite values.
Results may differ from the reference program's by a relative error of at most 0.02.
Values may be sent and summed in bfloat16 or wider, within the bound.
No kernel may reach another device: no remote copies, remote signals or barrier semaphores. Data moves between devices by JAX's collectives and lax.ppermute only.
A program may use at most 192 MiB of HBM per device.

```python
import functools
import math
import jax
import jax.numpy as jnp
import numpy as np
from jax import lax

D = 1024
HEADS = 16
KV_HEADS = 8
HEAD = 64
EXPERTS = 32
FF = 512
TOP = 8
TOK_DEV = 256
DOCS = 4
SEQS = 32
CAPACITY = 64


def draw_pad_mask(key, part):
    tail_most = TOK_DEV // 4
    tail_sizes = jax.random.randint(jax.random.fold_in(key, 11), (SEQS,), 0, tail_most + 1)
    chosen_row = jax.random.randint(jax.random.fold_in(key, 12), (), 0, SEQS)
    tail_sizes = jnp.where(jnp.arange(SEQS) == chosen_row, tail_most, tail_sizes)
    positions = jnp.arange(TOK_DEV)[None, :]
    return (positions < TOK_DEV - tail_sizes[:, None]).astype(jnp.int32)


def steps_of(stream_key, dims, shards, smallest, top_value):
    loudness, own = 1.0, jax.random.fold_in(stream_key, 6)
    for position, shards_of in shards:
        draws = jnp.exp(jax.random.uniform(jax.random.fold_in(own, position), (shards_of,), jnp.float32, smallest / len(shards), top_value / len(shards)))
        loudness = loudness * jnp.repeat(draws, dims[position] // shards_of).reshape([-1 if axis == position else 1 for axis in range(len(dims))])
    return loudness


def different_ones(stream_key, rows, number_of, top, lift):
    sequence = jax.random.permutation(jax.random.fold_in(stream_key, 1), number_of)
    pull = sequence
    for power in range(3):
        pull = pull * pull // number_of
    pull = pull * lift // number_of
    tickets = jax.random.randint(jax.random.fold_in(stream_key, 2), (rows, number_of), 0, 4096) + pull
    holders = jax.random.permutation(jax.random.fold_in(stream_key, 3), rows)[jnp.arange(number_of) % rows]
    tickets = jnp.where(jnp.arange(rows)[:, None] == holders[None, :], 1 << 14, tickets)
    score = tickets * number_of + jnp.arange(number_of)
    return lax.top_k(score.astype(jnp.int32), top)[1].astype(jnp.int32)


def split_up(number_of, total, limit, skew):
    loads = [(1 << 20) // math.isqrt(standing ** skew) + 1 for standing in range(2, number_of + 1)]
    rest, counts = total - limit - (number_of - 1), [1] * (number_of - 1)
    while rest > 0:
        candidates = [i for i in range(number_of - 1) if counts[i] < limit]
        mass, budget = sum([loads[i] for i in candidates]), rest
        for i in candidates:
            extra = min(limit - counts[i], max(1, budget * loads[i] // mass), rest)
            counts[i] = counts[i] + extra
            rest = rest - extra
    return np.array([limit] + counts)


def ragged_sizes(rng, number_of, total, bound, lean):
    if number_of == 2:
        one = jax.random.randint(rng, (), max(1, total - bound), min(bound, total - 1) + 1)
        return jnp.stack([one, total - one])
    lengths = jnp.asarray(split_up(number_of, total, bound, lean), jnp.int32)
    pairs = (number_of - 1) // 2
    giver, receiver = lengths[1:1 + 2 * pairs:2], lengths[2:2 + 2 * pairs:2]
    slack = jnp.minimum(giver - 1, bound - receiver)
    moved = jax.random.randint(jax.random.fold_in(rng, 1), (pairs,), 0, 1 << 20) % (slack + 1)
    lengths = lengths.at[1:1 + 2 * pairs:2].set(giver - moved).at[2:2 + 2 * pairs:2].set(receiver + moved)
    return lengths[jax.random.permutation(jax.random.fold_in(rng, 2), number_of)]


def normal_values(stream_key, dims, width, bound, pieces=(), held_as=jnp.bfloat16):
    values = width * jax.random.normal(stream_key, dims, jnp.float32)
    if pieces:
        values = values * steps_of(stream_key, dims, pieces, -0.22, 0.18)
    return jnp.clip(values, -bound, bound).astype(held_as)


def setup_inputs(seed: int = 0) -> dict:
    keys = jax.random.split(jax.random.key(seed), 17)
    hidden_in = normal_values(keys[0], (SEQS, TOK_DEV, D), 1.0, 6.0, ((0, 32),))
    segment_ids = jax.vmap(lambda own: jnp.searchsorted(jnp.cumsum(ragged_sizes(own, DOCS, TOK_DEV, TOK_DEV // 2, 1)), jnp.arange(TOK_DEV), side="right"))(jax.random.split(keys[1], SEQS)).reshape((SEQS, TOK_DEV)).astype(jnp.int32)
    pad_mask = draw_pad_mask(jax.random.fold_in(keys[16], 71), 0)
    expert_choice = different_ones(keys[3], SEQS * TOK_DEV, EXPERTS, TOP, 2048).reshape((SEQS, TOK_DEV, TOP))
    slot_rank = jax.vmap(lambda own: jax.random.permutation(own, TOK_DEV))(jax.random.split(keys[4], SEQS)).reshape((SEQS, TOK_DEV)).astype(jnp.int32)
    attn_gain = jnp.clip(1.0 + 0.1 * jax.random.normal(keys[5], (D,), jnp.float32), 0.5, 1.5).astype(jnp.bfloat16)
    query_weight = normal_values(keys[6], (D, HEADS * HEAD), D ** -0.5, 0.1875, ((0, 4),))
    key_weight = normal_values(keys[7], (D, KV_HEADS * HEAD), D ** -0.5, 0.1875, ((0, 4),))
    value_weight = normal_values(keys[8], (D, KV_HEADS * HEAD), D ** -0.5, 0.1875, ((0, 4),))
    output_weight = normal_values(keys[9], (HEADS * HEAD, D), (HEADS * HEAD * 8 // TOK_DEV) ** -0.5, 1.0, ((0, 4),))
    moe_gain = jnp.clip(1.0 + 0.1 * jax.random.normal(keys[10], (D,), jnp.float32), 0.5, 1.5).astype(jnp.bfloat16)
    router_weight = normal_values(keys[11], (D, EXPERTS), (0.5 * D ** -0.5), 0.25, ((0, 4),))
    gate_weight = normal_values(keys[12], (EXPERTS, D, FF), D ** -0.5, 0.1875, ((0, 8),))
    up_weight = normal_values(keys[13], (EXPERTS, D, FF), D ** -0.5, 0.1875, ((0, 8),))
    down_weight = normal_values(keys[14], (EXPERTS, FF, D), (FF // 16) ** -0.5, 1.0, ((0, 8),))
    out_grad = normal_values(keys[15], (SEQS, TOK_DEV, D), 1.0, 6.0, ((0, 32),))
    return dict(hidden_in=hidden_in, segment_ids=segment_ids, pad_mask=pad_mask, expert_choice=expert_choice, slot_rank=slot_rank, attn_gain=attn_gain, query_weight=query_weight, key_weight=key_weight, value_weight=value_weight, output_weight=output_weight, moe_gain=moe_gain, router_weight=router_weight, gate_weight=gate_weight, up_weight=up_weight, down_weight=down_weight, out_grad=out_grad)


eps = 1e-05
masked = -1e+30
highest = lax.Precision.HIGHEST

@jax.custom_vjp
def low(v):
    return lax.optimization_barrier(v.astype(jnp.bfloat16)).astype(jnp.float32)

@jax.custom_vjp
def low_back(v):
    return v

def low_keep(v):
    return (low(v), None)

def low_pass(kept, grad):
    return (grad,)

def back_keep(v):
    return (v, None)

def back_low(kept, grad):
    return (low(grad),)
low.defvjp(low_keep, low_pass)
low_back.defvjp(back_keep, back_low)

def rope_tables(segments):
    length = segments.shape[0]
    positions = jnp.arange(length, dtype=jnp.int32)
    starts = jnp.concatenate([jnp.ones((1,), dtype=bool), segments[1:] != segments[:-1]])
    doc_start = lax.cummax(jnp.where(starts, positions, 0), axis=0)
    places = (positions - doc_start).astype(jnp.float32)
    half_size = HEAD // 2
    frequency = 10000.0 ** (-jnp.arange(half_size, dtype=jnp.float32) * 2.0 / HEAD)
    angles = places[:, None] * frequency[None, :]
    cosine = jnp.concatenate([jnp.cos(angles), jnp.cos(angles)], -1)
    sine_table = jnp.concatenate([jnp.sin(angles), jnp.sin(angles)], -1)
    return (cosine, sine_table)

def rotate(values, cosine, sine_table):
    half_size = values.shape[-1] // 2
    turned = jnp.concatenate([-values[..., half_size:], values[..., :half_size]], -1)
    return values * cosine[:, None, :] + turned * sine_table[:, None, :]

def allowed_mask(segments, live_int):
    length = segments.shape[0]
    rows_idx = jnp.arange(length, dtype=jnp.int32)[:, None]
    cols_idx = jnp.arange(length, dtype=jnp.int32)[None, :]
    same_doc = segments[:, None] == segments[None, :]
    return same_doc & (cols_idx <= rows_idx) & (live_int[None, :] > 0) | (cols_idx == rows_idx)

def softmax_rows(values):
    shifted = values - lax.optimization_barrier(jnp.max(values, -1, keepdims=True))
    powers = jnp.exp(shifted)
    return powers / lax.optimization_barrier(jnp.sum(powers, -1, keepdims=True))

def one_sequence(params, hidden, live_int, segments, choices, ranks):
    gain_one, query_w, key_w, value_w, output_w, gain_two, router_w, gate_w, up_w, down_w = params
    length = hidden.shape[0]
    live = live_int.astype(jnp.float32)
    inv_one = lax.rsqrt(lax.optimization_barrier(jnp.mean(hidden * hidden, -1, keepdims=True)) + eps)
    attn_in = low(hidden * inv_one * gain_one)
    cosine, sine_table = rope_tables(segments)
    query_raw = low_back(jnp.dot(attn_in, query_w, precision=highest))
    query_rot = low(rotate(query_raw.reshape(length, HEADS, HEAD), cosine, sine_table))
    query_rot = query_rot.reshape(length, KV_HEADS, HEADS // KV_HEADS, HEAD)
    key_raw = low_back(jnp.dot(attn_in, key_w, precision=highest))
    key_rot = low(rotate(key_raw.reshape(length, KV_HEADS, HEAD), cosine, sine_table))
    value_rows = low(low_back(jnp.dot(attn_in, value_w, precision=highest))).reshape(length, KV_HEADS, HEAD)
    scores = low_back(jnp.einsum('qgrd,kgd->grqk', query_rot, key_rot, precision=highest) * HEAD ** (-0.5))
    allowed = allowed_mask(segments, live_int)
    scores = jnp.where(allowed[None, None], scores, masked)
    probs = softmax_rows(scores)
    mixed = jnp.einsum('grqk,kgd->qgrd', low(probs), value_rows, precision=highest)
    attn_out = low(low_back(mixed)).reshape(length, HEADS * HEAD)
    resid_one = hidden + low_back(jnp.dot(attn_out, output_w, precision=highest))
    inv_two = lax.rsqrt(lax.optimization_barrier(jnp.mean(resid_one * resid_one, -1, keepdims=True)) + eps)
    moe_in = low(resid_one * inv_two * gain_two)
    logits = low_back(jnp.dot(moe_in, router_w, precision=highest))
    picked = choices[:, :, None] == jnp.arange(EXPERTS, dtype=jnp.int32)[None, None, :]
    chosen = lax.optimization_barrier(jnp.sum(jnp.where(picked, logits[:, None, :], 0.0), -1))
    gates = softmax_rows(chosen)
    active = (lax.optimization_barrier(jnp.sum(picked.astype(jnp.int32), 1)) * live_int[:, None]).astype(jnp.int32)
    by_rank = jnp.zeros_like(active).at[ranks].set(active)
    earlier = (jnp.cumsum(by_rank, 0) - by_rank).astype(jnp.int32)
    place_all = earlier[ranks]
    places = lax.optimization_barrier(jnp.sum(jnp.where(picked, place_all[:, None, :], 0), -1)).astype(jnp.int32)
    kept = (live_int[:, None] > 0) & (places < CAPACITY)
    routed = (picked & kept[:, :, None]).astype(jnp.float32)
    slot_hot = (places[:, :, None] == jnp.arange(CAPACITY, dtype=jnp.int32)[None, None, :]).astype(jnp.float32)
    dispatch = jnp.einsum('lke,lkc->ecl', routed, slot_hot, precision=highest)
    gate_table = lax.optimization_barrier(jnp.sum(routed * gates[:, :, None], 1))
    combine = dispatch * jnp.transpose(gate_table)[:, None, :]
    expert_rows = low_back(jnp.einsum('ecl,ld->ecd', dispatch, moe_in, precision=highest))
    gate_pre = low_back(jnp.einsum('ecd,edf->ecf', expert_rows, gate_w, precision=highest))
    up_pre = low_back(jnp.einsum('ecd,edf->ecf', expert_rows, up_w, precision=highest))
    act = low(gate_pre * jax.nn.sigmoid(gate_pre) * up_pre)
    expert_out = low(low_back(jnp.einsum('ecf,efd->ecd', act, down_w, precision=highest)))
    moe_branch = jnp.einsum('ecl,ecd->ld', combine, expert_out, precision=highest)
    return live[:, None] * (resid_one + moe_branch)

def reference(hidden_in, segment_ids, pad_mask, expert_choice, slot_rank, attn_gain, query_weight, key_weight, value_weight, output_weight, moe_gain, router_weight, gate_weight, up_weight, down_weight, out_grad):
    group_size = math.gcd(SEQS, max(1, 4096 // TOK_DEV))

    def regroup(array):
        return array.reshape((SEQS // group_size, group_size) + array.shape[1:])
    int_parts = (regroup(pad_mask), regroup(segment_ids), regroup(expert_choice), regroup(slot_rank))
    params = tuple((weight.astype(jnp.float32) for weight in (attn_gain, query_weight, key_weight, value_weight, output_weight, moe_gain, router_weight, gate_weight, up_weight, down_weight)))

    def forward(hidden_all, params_all):

        def per_group(packed):
            return jax.vmap(functools.partial(one_sequence, params_all))(*packed)
        result = lax.map(jax.checkpoint(per_group), (regroup(hidden_all),) + int_parts)
        return result.reshape(hidden_all.shape)
    outputs, pullback = jax.vjp(forward, hidden_in.astype(jnp.float32), params)
    hidden_grad, param_grads = pullback(out_grad.astype(jnp.float32))
    return (outputs.astype(jnp.bfloat16), hidden_grad.astype(jnp.bfloat16), param_grads[0], param_grads[1], param_grads[2], param_grads[3], param_grads[4], param_grads[5], param_grads[6], param_grads[7], param_grads[8], param_grads[9])
```

```python
import jax
import jax.numpy as jnp
from jax import lax
from jax.sharding import PartitionSpec as P

HEADS = 16
KV_HEADS = 8
HEAD = 64

eps = 1e-05
masked = -1e30
f32 = jnp.float32
bf16 = jnp.bfloat16


def mm(spec, a, b):
    return jnp.einsum(spec, a, b, preferred_element_type=f32)


def rope_tables(segments, head_size):
    length = segments.shape[0]
    positions = jnp.arange(length, dtype=jnp.int32)
    doc_start = jnp.sum((segments[None, :] < segments[:, None]).astype(jnp.int32), -1)
    places = (positions - doc_start).astype(f32)
    half_size = head_size // 2
    frequency = 10000.0 ** (-jnp.arange(half_size, dtype=f32) * 2.0 / head_size)
    angles = places[:, None] * frequency[None, :]
    cosine = jnp.concatenate([jnp.cos(angles), jnp.cos(angles)], -1)
    sine_table = jnp.concatenate([jnp.sin(angles), jnp.sin(angles)], -1)
    return (cosine, sine_table)


def rotate(values, cosine, sine_table):
    half_size = values.shape[-1] // 2
    turned = jnp.concatenate([-values[..., half_size:], values[..., :half_size]], -1)
    return values * cosine[:, None, :] + turned * sine_table[:, None, :]


def unrotate(grads, cosine, sine_table):
    half_size = grads.shape[-1] // 2
    scaled = grads * sine_table[:, None, :]
    turned = jnp.concatenate([scaled[..., half_size:], -scaled[..., :half_size]], -1)
    return grads * cosine[:, None, :] + turned


def allowed_mask(segments, live_int):
    length = segments.shape[0]
    rows_idx = jnp.arange(length, dtype=jnp.int32)[:, None]
    cols_idx = jnp.arange(length, dtype=jnp.int32)[None, :]
    same_doc = segments[:, None] == segments[None, :]
    return same_doc & (cols_idx <= rows_idx) & (live_int[None, :] > 0) | (cols_idx == rows_idx)


def norm_back(grad_in, normed, factor):
    return factor * (grad_in - normed * jnp.mean(grad_in * normed, -1, keepdims=True))


class Net:
    def __init__(self, owners, shards):
        self.owners, self.shards, self.levels = owners, shards, owners // 2
        self.square = shards == 4
        place = lax.axis_index("expert")
        self.owner, self.core, self.level = place, place % 2, place // 2
        self.shard = lax.axis_index("shard")

    def swap(self, x):
        return lax.ppermute(x, "expert", [(i, i ^ 1) for i in range(self.owners)])

    def lift(self, x, by):
        return lax.ppermute(
            x, "expert", [(i, (i + 2 * by) % self.owners) for i in range(self.owners)]
        )

    def flip(self, x, bits):
        return lax.ppermute(x, "shard", [(i, i ^ bits) for i in range(self.shards)])

    def over_expert(self, x):
        mine = jnp.stack([x] + [self.lift(x, k) for k in range(1, self.levels)])
        return mine, self.swap(mine)

    def home(self, mine, other):
        both = mine + self.swap(other.astype(bf16)).astype(f32)
        total = both[0]
        for k in range(1, self.levels):
            total = total + self.lift(both[k].astype(bf16), self.levels - k).astype(f32)
        return total

    def over_square(self, x):
        half = x.shape[0] // 2
        one, two = self.flip(x, 1), self.flip(x, 2)
        three = jnp.concatenate([self.flip(two[:half], 1), self.flip(one[half:], 2)], 0)
        return one, two, three

    def gather_rows(self, x):
        if not self.square:
            return lax.all_gather(x, "shard", axis=0, tiled=True)
        rows = x.shape[0] // 2
        half = lax.dynamic_slice_in_dim(x, self.core * rows, rows, 0)
        rel = jnp.stack((half,) + self.over_square(half))
        other = self.swap(rel)
        low = jnp.where(self.core == 0, rel, other)
        high = jnp.where(self.core == 0, other, rel)
        full = jnp.stack([low, high], 1)
        full = full[jnp.arange(self.shards) ^ self.shard]
        return full.reshape((self.shards * x.shape[0],) + x.shape[1:])

    def sum_rows(self, x):
        if not self.square:
            part = lax.psum_scatter(x.astype(bf16), "shard", scatter_dimension=0, tiled=True)
            return lax.psum(part, "expert").astype(f32)
        rows = x.shape[0] // self.shards // 2
        wide = x.shape[1]
        blocks = x.reshape(self.shards, 2, rows, wide)[jnp.arange(self.shards) ^ self.shard]
        mine = lax.dynamic_index_in_dim(blocks, self.core, 1, False)
        other = lax.dynamic_index_in_dim(blocks, 1 - self.core, 1, False)
        chip = mine + self.swap(other.astype(bf16)).astype(f32)
        cut = wide // 256 * 128
        ends = []
        for part, first, second in ((chip[..., :cut], 1, 2), (chip[..., cut:], 2, 1)):
            near, far = self.flip(part[first].astype(bf16), first), self.flip(part[3].astype(bf16), first)
            last = self.flip((part[second] + far.astype(f32)).astype(bf16), second)
            ends.append(part[0] + near.astype(f32) + last.astype(f32))
        own = jnp.concatenate(ends, 1)
        levels = self.levels
        parts = own.reshape(levels, rows // levels, wide)
        part_of = lambda at: lax.dynamic_index_in_dim(parts, at % levels, 0, False)
        total = part_of(self.level)
        for k in range(1, levels):
            total = total + self.lift(part_of(self.level + k).astype(bf16), k).astype(f32)
        total = total.astype(bf16)
        found = jnp.stack([total] + [self.lift(total, k) for k in range(1, levels)])
        found = found[(self.level - jnp.arange(levels)) % levels].reshape(rows, wide)
        twin = self.swap(found)
        low = jnp.where(self.core == 0, found, twin)
        high = jnp.where(self.core == 0, twin, found)
        return jnp.concatenate([low, high], 0).astype(f32)


def per_device(
    hidden_in,
    segment_ids,
    pad_mask,
    expert_choice,
    slot_rank,
    attn_gain,
    query_weight,
    key_weight,
    value_weight,
    output_weight,
    moe_gain,
    router_weight,
    gate_weight,
    up_weight,
    down_weight,
    out_grad,
):
    owners, shards = lax.axis_size("expert"), lax.axis_size("shard")
    net = Net(owners, shards)
    hidden = hidden_in[0].astype(f32)
    length, width = hidden.shape
    segments = segment_ids[0]
    live_int = pad_mask[0]
    live = live_int.astype(f32)
    choices = expert_choice[0]
    ranks = slot_rank[0]
    top_count = choices.shape[1]
    local_experts = gate_weight.shape[0]
    experts_all = owners * local_experts
    capacity = length * top_count // experts_all
    slots = local_experts * capacity
    kv_groups = HEADS // KV_HEADS
    score_scale = HEAD ** (-0.5)
    heads_wide, kv_wide = HEADS * HEAD, KV_HEADS * HEAD

    ids = jnp.arange(experts_all, dtype=jnp.int32)
    picked = jnp.any(choices.T[:, None, :] == ids[None, :, None], 0)
    active = (picked & (live_int > 0)[None, :]).astype(bf16)
    earlier = (ranks[:, None] < ranks[None, :]).astype(bf16)
    places = mm("et,tu->eu", active, earlier)
    kept = picked & (live_int > 0)[None, :] & (places < capacity)
    codes = jnp.where(kept, places, -1.0).astype(bf16)

    tail_wide = local_experts * length

    def tail_row(values):
        return jnp.pad(values.reshape(-1, tail_wide), ((0, 0), (0, width - tail_wide)))

    def with_tail(rows, first, second):
        return jnp.concatenate([rows, tail_row(first), tail_row(second)], 0)

    grad_two = (live[:, None] * out_grad[0].astype(f32)).astype(bf16)
    grad_block = with_tail(grad_two, codes, jnp.zeros_like(codes))
    grad_mine, grad_other = net.over_expert(grad_block)

    misc = jnp.concatenate(
        [router_weight, attn_gain[:, None], moe_gain[:, None]], 1
    )
    misc = jnp.pad(misc, ((0, 0), (0, 128 - misc.shape[1])))
    full = net.gather_rows(
        jnp.concatenate([query_weight, key_weight, value_weight, output_weight, misc], 1)
    )
    cuts = [heads_wide, heads_wide + kv_wide, heads_wide + 2 * kv_wide]
    query_full, key_full, value_full, output_full, misc = jnp.split(
        full, cuts + [cuts[-1] + width], 1
    )
    router_full = misc[:, :experts_all]
    gain_one = misc[:, experts_all].astype(f32)
    gain_two = misc[:, experts_all + 1].astype(f32)

    inv_one = lax.rsqrt(jnp.mean(hidden * hidden, -1, keepdims=True) + eps)
    normed_one = hidden * inv_one
    attn_in = (normed_one * gain_one).astype(bf16)
    cosine, sine_table = rope_tables(segments, HEAD)
    query_raw = jnp.dot(attn_in, query_full, preferred_element_type=f32)
    query_rot = (
        rotate(query_raw.reshape(length, HEADS, HEAD), cosine, sine_table)
        .astype(bf16)
        .reshape(length, KV_HEADS, kv_groups, HEAD)
    )
    key_raw = jnp.dot(attn_in, key_full, preferred_element_type=f32)
    key_rot = rotate(key_raw.reshape(length, KV_HEADS, HEAD), cosine, sine_table).astype(bf16)
    value_rows = (
        jnp.dot(attn_in, value_full, preferred_element_type=f32)
        .astype(bf16)
        .reshape(length, KV_HEADS, HEAD)
    )
    allowed = allowed_mask(segments, live_int)

    def score_block():
        raw_scores = mm("qgrd,kgd->grqk", query_rot, key_rot) * score_scale
        return jnp.where(allowed[None, None], raw_scores, masked)

    scores = score_block()
    top_score = jnp.max(scores, -1, keepdims=True)
    log_total = top_score + jnp.log(jnp.sum(jnp.exp(scores - top_score), -1, keepdims=True))
    probs = jnp.exp(scores - log_total)
    mixed = mm("grqk,kgd->qgrd", probs.astype(bf16), value_rows)
    attn_out = mixed.astype(bf16).reshape(length, heads_wide)
    resid_one = hidden + jnp.dot(attn_out, output_full, preferred_element_type=f32)
    inv_two = lax.rsqrt(jnp.mean(resid_one * resid_one, -1, keepdims=True) + eps)
    normed_two = resid_one * inv_two
    moe_in = (normed_two * gain_two).astype(bf16)
    logits = mm("de,td->et", router_full, moe_in)
    top_logit = jnp.max(jnp.where(picked, logits, masked), 0, keepdims=True)
    powers = jnp.where(picked, jnp.exp(jnp.minimum(logits - top_logit, 0.0)), 0.0)
    gates = powers / jnp.sum(powers, 0, keepdims=True)
    gates_kept = jnp.where(kept, gates, 0.0)
    gates_high = gates_kept.astype(bf16)
    gates_low = (gates_kept - gates_high.astype(f32)).astype(bf16)
    row_block = with_tail(moe_in, gates_high, gates_low)
    rows_mine, rows_other = net.over_expert(row_block)

    own_row = (jnp.arange(owners) == net.owner).astype(f32)

    def tail_of(block, at):
        rows = block[:, length + at * owners : length + (at + 1) * owners].astype(f32)
        row = jnp.sum(rows * own_row[None, :, None], 1)[:, :tail_wide]
        return row.reshape(-1, local_experts, 1, length)

    def column(rows, grads, data_path):
        count = rows.shape[0]
        code = tail_of(grads, 0)
        gate = tail_of(rows, 0) + tail_of(rows, 1)
        slot_ids = jnp.arange(capacity, dtype=jnp.int32).astype(f32)[None, None, :, None]
        hot = code == slot_ids
        slot_gate = jnp.sum(jnp.where(hot, gate, 0.0), -1, keepdims=True)
        pick = hot.astype(bf16).reshape(count, slots, length)
        shape = (count, local_experts, capacity, width)
        taken = mm("sqt,std->sqd", pick, rows[:, :length]).astype(bf16).reshape(shape)
        grad_rows = mm("sqt,std->sqd", pick, grads[:, :length]).astype(bf16).reshape(shape)
        gate_pre = mm("secd,edf->secf", taken, gate_weight)
        up_pre = mm("secd,edf->secf", taken, up_weight)
        sigma = jax.nn.sigmoid(gate_pre)
        silu_vals = gate_pre * sigma
        act = (silu_vals * up_pre).astype(bf16)
        raw_grads = mm("secd,efd->secf", grad_rows, down_weight)
        act_grads = raw_grads * slot_gate
        gate_pre_grads = (act_grads * up_pre * sigma * (1.0 + gate_pre * (1.0 - sigma))).astype(bf16)
        up_pre_grads = (act_grads * silu_vals).astype(bf16)
        act_scaled = (act.astype(f32) * slot_gate).astype(bf16)
        terms = (
            mm("secd,secf->edf", taken, gate_pre_grads),
            mm("secd,secf->edf", taken, up_pre_grads),
            mm("secf,secd->efd", act_scaled, grad_rows),
        )
        if not data_path:
            return terms
        gate_grads = jnp.sum(act.astype(f32) * raw_grads, -1, keepdims=True)
        gate_grads = jnp.sum(jnp.where(hot, gate_grads, 0.0), 2)
        gate_grads = tail_row(gate_grads).reshape(count, 1, width) * own_row[None, :, None]
        high = gate_grads.astype(bf16)
        low = (gate_grads - high.astype(f32)).astype(bf16)
        outs = mm("secf,efd->secd", act, down_weight)
        outs = (outs * slot_gate).astype(bf16).reshape(count, slots, width)
        branch = mm("sqt,sqd->std", pick, outs)
        back = mm("secf,edf->secd", gate_pre_grads, gate_weight)
        back = (back + mm("secf,edf->secd", up_pre_grads, up_weight)).astype(bf16)
        back = mm("sqt,sqd->std", pick, back.reshape(count, slots, width))
        back = jnp.concatenate([back, high.astype(f32), low.astype(f32)], 1)
        return terms, branch, back

    rows_all = jnp.concatenate([rows_mine, rows_other], 0)
    grads_all = jnp.concatenate([grad_mine, grad_other], 0)
    terms, branch, back = column(rows_all, grads_all, True)
    levels = net.levels
    back = net.home(back[:levels], back[levels:])
    branch = net.home(branch[:levels], branch[levels:])
    if net.square:
        near_rows, near_grads = net.over_square(rows_mine), net.over_square(grad_mine)
        for rows, grads in zip(near_rows, near_grads):
            rows = jnp.concatenate([rows, net.swap(rows)], 0)
            grads = jnp.concatenate([grads, net.swap(grads)], 0)
            more = column(rows, grads, False)
            terms = tuple(a + b for a, b in zip(terms, more))
    else:
        terms = tuple(lax.psum(a.astype(bf16), "shard").astype(f32) for a in terms)

    block_out = (live[:, None] * (resid_one + branch)).astype(bf16)
    gate_grads = back[length : length + owners] + back[length + owners :]
    gate_grads = gate_grads[:, :tail_wide].reshape(experts_all, length)
    gate_inner = jnp.sum(gates * gate_grads, 0, keepdims=True)
    logit_grads = (gates * (gate_grads - gate_inner)).astype(bf16)
    router_grad = mm("td,et->de", moe_in, logit_grads)
    moe_in_grads = back[:length] + mm("et,de->td", logit_grads, router_full)
    gain_two_grad = jnp.sum(moe_in_grads * normed_two, 0)
    resid_grad = grad_two.astype(f32) + norm_back(moe_in_grads * gain_two, normed_two, inv_two)
    branch_grad = resid_grad.astype(bf16)
    output_grad_w = mm("lh,ld->hd", attn_out, branch_grad)
    mixed_grad = mm("ld,hd->lh", branch_grad, output_full)
    mixed_grad = mixed_grad.astype(bf16).reshape(length, KV_HEADS, kv_groups, HEAD)
    probs_again = jnp.exp(score_block() - log_total)
    prob_grads = mm("qgrd,kgd->grqk", mixed_grad, value_rows)
    value_grad = mm("grqk,qgrd->kgd", probs_again.astype(bf16), mixed_grad)
    value_grad = value_grad.astype(bf16).reshape(length, kv_wide)
    score_grads = (
        probs_again * (prob_grads - jnp.sum(probs_again * prob_grads, -1, keepdims=True))
    ).astype(bf16)
    query_rot_grad = mm("grqk,kgd->qgrd", score_grads, key_rot) * score_scale
    key_rot_grad = mm("grqk,qgrd->kgd", score_grads, query_rot) * score_scale
    query_grad = (
        unrotate(query_rot_grad.reshape(length, HEADS, HEAD), cosine, sine_table)
        .astype(bf16)
        .reshape(length, heads_wide)
    )
    key_grad = unrotate(key_rot_grad, cosine, sine_table).astype(bf16).reshape(length, kv_wide)
    query_grad_w = mm("ld,lh->dh", attn_in, query_grad)
    key_grad_w = mm("ld,lh->dh", attn_in, key_grad)
    value_grad_w = mm("ld,lh->dh", attn_in, value_grad)
    attn_in_grads = mm("lh,dh->ld", query_grad, query_full)
    attn_in_grads = attn_in_grads + mm("lh,dh->ld", key_grad, key_full)
    attn_in_grads = attn_in_grads + mm("lh,dh->ld", value_grad, value_full)
    gain_one_grad = jnp.sum(attn_in_grads * normed_one, 0)
    hidden_grad = resid_grad + norm_back(attn_in_grads * gain_one, normed_one, inv_one)
    misc_grad = jnp.concatenate([router_grad, gain_one_grad[:, None], gain_two_grad[:, None]], 1)
    misc_grad = jnp.pad(misc_grad, ((0, 0), (0, 128 - misc_grad.shape[1])))
    sums = net.sum_rows(
        jnp.concatenate([query_grad_w, key_grad_w, value_grad_w, output_grad_w, misc_grad], 1)
    )
    sum_query, sum_key, sum_value, sum_output, sum_misc = jnp.split(
        sums, cuts + [cuts[-1] + width], 1
    )
    return (
        block_out[None],
        hidden_grad.astype(bf16)[None],
        sum_misc[:, experts_all],
        sum_query,
        sum_key,
        sum_value,
        sum_output,
        sum_misc[:, experts_all + 1],
        sum_misc[:, :experts_all],
        terms[0],
        terms[1],
        terms[2],
    )


def solution(mesh):
    tokens = ("expert", "shard")
    in_specs = (
        P(tokens, None, None),
        P(tokens, None),
        P(tokens, None),
        P(tokens, None, None),
        P(tokens, None),
        P("shard"),
        P("shard", None),
        P("shard", None),
        P("shard", None),
        P("shard", None),
        P("shard"),
        P("shard", None),
        P("expert", None, None),
        P("expert", None, None),
        P("expert", None, None),
        P(tokens, None, None),
    )
    out_specs = (
        P(tokens, None, None),
        P(tokens, None, None),
        P("shard"),
        P("shard", None),
        P("shard", None),
        P("shard", None),
        P("shard", None),
        P("shard"),
        P("shard", None),
        P("expert", None, None),
        P("expert", None, None),
        P("expert", None, None),
    )
    return jax.shard_map(
        per_device, mesh=mesh, in_specs=in_specs, out_specs=out_specs, check_vma=False
    )
```

```python
import functools

import jax
import jax.numpy as jnp
from jax import lax
from jax.experimental import pallas as pl
from jax.experimental.pallas import tpu as pltpu
from jax.sharding import PartitionSpec as P

HEADS = 16
KV_HEADS = 8
HEAD = 64

eps = 1e-05
masked = -1e30
f32 = jnp.float32
bf16 = jnp.bfloat16


def mm(spec, a, b):
    return jnp.einsum(spec, a, b, preferred_element_type=f32)


def rope_tables(segments, head_size):
    length = segments.shape[0]
    positions = jnp.arange(length, dtype=jnp.int32)
    doc_start = jnp.sum((segments[None, :] < segments[:, None]).astype(jnp.int32), -1)
    places = (positions - doc_start).astype(f32)
    half_size = head_size // 2
    frequency = 10000.0 ** (-jnp.arange(half_size, dtype=f32) * 2.0 / head_size)
    angles = places[:, None] * frequency[None, :]
    cosine = jnp.concatenate([jnp.cos(angles), jnp.cos(angles)], -1)
    sine_table = jnp.concatenate([jnp.sin(angles), jnp.sin(angles)], -1)
    return (cosine, sine_table)


def rotate(values, cosine, sine_table):
    half_size = values.shape[-1] // 2
    turned = jnp.concatenate([-values[..., half_size:], values[..., :half_size]], -1)
    return values * cosine[:, None, :] + turned * sine_table[:, None, :]


def unrotate(grads, cosine, sine_table):
    half_size = grads.shape[-1] // 2
    scaled = grads * sine_table[:, None, :]
    turned = jnp.concatenate([scaled[..., half_size:], -scaled[..., :half_size]], -1)
    return grads * cosine[:, None, :] + turned


def allowed_mask(segments, live_int):
    length = segments.shape[0]
    rows_idx = jnp.arange(length, dtype=jnp.int32)[:, None]
    cols_idx = jnp.arange(length, dtype=jnp.int32)[None, :]
    same_doc = segments[:, None] == segments[None, :]
    return same_doc & (cols_idx <= rows_idx) & (live_int[None, :] > 0) | (cols_idx == rows_idx)


def norm_back(grad_in, normed, factor):
    return factor * (grad_in - normed * jnp.mean(grad_in * normed, -1, keepdims=True))


def prepare(refs, owner_ref, picks, gates, taken, grad_rows, sizes):
    length, owners, local, capacity = sizes
    owner = owner_ref[0]
    width = taken.shape[-1]
    span = local * length
    at = 0
    for rows_ref, grads_ref in refs:

        def one(block, carry, rows_ref=rows_ref, grads_ref=grads_ref, at=at):
            ids = lax.broadcasted_iota(jnp.int32, (owners, width), 0)

            def tail(ref, part):
                tail_rows = ref[block, pl.ds(length + part * owners, owners), :].astype(f32)
                return jnp.sum(jnp.where(ids == owner, tail_rows, 0.0), 0, keepdims=True)

            code = tail(grads_ref, 0)
            gate = tail(rows_ref, 0) + tail(rows_ref, 1)
            slot_ids = lax.broadcasted_iota(jnp.int32, (capacity, length), 0).astype(f32)
            for e in range(local):
                part = slice(e * length, (e + 1) * length)
                hot = code[:, part] == slot_ids
                slot_gate = jnp.sum(jnp.where(hot, gate[:, part], 0.0), -1, keepdims=True)
                here = slice(e * capacity, (e + 1) * capacity)
                picks[at + block, here, :] = jnp.where(hot, 1.0, 0.0).astype(bf16)
                gates[at + block, here, :] = jnp.broadcast_to(slot_gate, (capacity, 128))
            pick = picks[at + block]
            rows = rows_ref[block, pl.ds(0, length), :]
            taken[at + block] = jnp.dot(pick, rows, preferred_element_type=f32).astype(bf16)
            rows = grads_ref[block, pl.ds(0, length), :]
            grad_rows[at + block] = jnp.dot(pick, rows, preferred_element_type=f32).astype(bf16)
            return carry

        lax.fori_loop(0, rows_ref.shape[0], one, 0)
        at += rows_ref.shape[0]


def dot_nt(a, b):
    return lax.dot_general(a, b, (((1,), (1,)), ((), ())), preferred_element_type=f32)


def dot_tn(a, b):
    return lax.dot_general(a, b, (((0,), (0,)), ((), ())), preferred_element_type=f32)


def hidden_units(rows, grads, gate, gate_w, up_w, down_w):
    gate_pre = jnp.dot(rows, gate_w, preferred_element_type=f32)
    up_pre = jnp.dot(rows, up_w, preferred_element_type=f32)
    raw_grads = dot_nt(grads, down_w)
    sigma = jax.nn.sigmoid(gate_pre)
    silu_vals = gate_pre * sigma
    act = (silu_vals * up_pre).astype(bf16)
    act_grads = raw_grads * gate
    gate_pre_grads = (act_grads * up_pre * (sigma + silu_vals * (1.0 - sigma))).astype(bf16)
    up_pre_grads = (act_grads * silu_vals).astype(bf16)
    return act, raw_grads, gate_pre_grads, up_pre_grads


def whole(shape):
    zeros = (0,) * len(shape)
    return pl.BlockSpec(shape, lambda e, _: zeros, pipeline_mode=pl.Buffered(1))


def per_expert(shape):
    zeros = (0,) * len(shape)
    return pl.BlockSpec((1,) + shape, lambda e, _: (e,) + zeros)


def data_kernel(owner_ref, rows_a, rows_b, grads_a, grads_b, gate_w, up_w, down_w,
                branch_a, branch_b, back_a, back_b, token, picks, gates, taken, grad_rows, inner,
                *, sizes):
    length, owners, local, capacity = sizes
    e = pl.program_id(0)
    count, width = taken.shape[0], taken.shape[-1]

    @pl.when(e == 0)
    def _():
        prepare(((rows_a, grads_a), (rows_b, grads_b)), owner_ref, picks, gates, taken, grad_rows, sizes)

    here = pl.ds(pl.multiple_of(e * capacity, capacity), capacity)
    rows = taken[:, here, :].reshape(count * capacity, width)
    grads = grad_rows[:, here, :].reshape(count * capacity, width)
    gate = gates[:, here, :][:, :, :1].reshape(count * capacity, 1)
    act, raw, gate_pre_grads, up_pre_grads = hidden_units(
        rows, grads, gate, gate_w[0], up_w[0], down_w[0]
    )
    gate_grads = jnp.sum(act.astype(f32) * raw, -1, keepdims=True).reshape(count, capacity, 1)
    hot = picks[:, here, :].astype(f32)
    inner[e] = jnp.sum(hot * gate_grads, 1)
    outs = jnp.dot(act, down_w[0], preferred_element_type=f32) * gate
    grad_rows[:, here, :] = outs.astype(bf16).reshape(count, capacity, width)
    back = dot_nt(gate_pre_grads, gate_w[0]) + dot_nt(up_pre_grads, up_w[0])
    taken[:, here, :] = back.astype(bf16).reshape(count, capacity, width)

    @pl.when(e == local - 1)
    def _():
        token[...] = jnp.zeros_like(token)
        ids = lax.broadcasted_iota(jnp.int32, (owners, width), 0)
        at = 0
        for branch, back in ((branch_a, back_a), (branch_b, back_b)):

            def one(block, carry, branch=branch, back=back, at=at):
                pick = picks[at + block]
                branch[block] = dot_tn(pick, grad_rows[at + block]).astype(branch.dtype)
                back[block, pl.ds(0, length), :] = dot_tn(pick, taken[at + block]).astype(back.dtype)
                return carry

            lax.fori_loop(0, branch.shape[0], one, 0)
            for block in range(branch.shape[0]):
                row = [inner[i, at + block : at + block + 1, :] for i in range(local)]
                if local * length < width:
                    row.append(jnp.zeros((1, width - local * length), f32))
                row = jnp.concatenate(row, 1)
                high = row.astype(bf16)
                low = row - high.astype(f32)
                for part, value in ((0, high.astype(f32)), (1, low)):
                    value = jnp.where(ids == owner_ref[0], value, 0.0).astype(bf16)
                    back[block, pl.ds(length + part * owners, owners), :] = value.astype(back.dtype)
            at += branch.shape[0]


def data_path(owner, rows, grads, weights, sizes):
    length, owners, local, capacity = sizes
    (rows_a, rows_b), (grads_a, grads_b) = rows, grads
    half, tall, width = rows_a.shape
    hidden_wide = weights[0].shape[-1]
    count, slots = 2 * half, local * capacity
    flops = 2 * count * slots * width * (6 * hidden_wide + 4 * length)
    shapes = [(half, length, width)] * 2 + [(half, tall, width)] * 2
    kinds = [f32, bf16, f32, bf16]
    return pl.pallas_call(
        functools.partial(data_kernel, sizes=sizes),
        grid_spec=pltpu.PrefetchScalarGridSpec(
            num_scalar_prefetch=1,
            grid=(local,),
            in_specs=[whole(rows_a.shape)] * 4
            + [per_expert((width, hidden_wide))] * 2
            + [per_expert((hidden_wide, width))],
            out_specs=[whole(s) for s in shapes] + [whole((8, 128))],
            scratch_shapes=[
                pltpu.VMEM((count, slots, length), bf16),
                pltpu.VMEM((count, slots, 128), f32),
                pltpu.VMEM((count, slots, width), bf16),
                pltpu.VMEM((count, slots, width), bf16),
                pltpu.VMEM((local, count, length), f32),
            ],
        ),
        out_shape=[jax.ShapeDtypeStruct(s, k) for s, k in zip(shapes, kinds)]
        + [jax.ShapeDtypeStruct((8, 128), f32)],
        compiler_params=pltpu.CompilerParams(vmem_limit_bytes=62 * 2**20),
        cost_estimate=pl.CostEstimate(flops=flops, bytes_accessed=40 * 2**20, transcendentals=0),
        name="experts_data",
    )(owner, rows_a, rows_b, grads_a, grads_b, *weights)


def weight_kernel(owner_ref, *refs, blocks, sizes, more):
    length, owners, local, capacity = sizes
    pairs = [(refs[2 * i], refs[2 * i + 1]) for i in range(blocks)]
    refs = refs[2 * blocks :]
    gate_w, up_w, down_w = refs[:3]
    refs = refs[3 + 1 :]
    sums = refs[:3] if more else None
    refs = refs[3:] if more else refs
    gate_out, up_out, down_out, token, picks, gates, taken, grad_rows = refs
    e = pl.program_id(0)
    count, width = taken.shape[0], taken.shape[-1]

    @pl.when(e == 0)
    def _():
        token[...] = jnp.zeros_like(token)
        prepare(pairs, owner_ref, picks, gates, taken, grad_rows, sizes)

    here = pl.ds(pl.multiple_of(e * capacity, capacity), capacity)
    rows = taken[:, here, :].reshape(count * capacity, width)
    grads = grad_rows[:, here, :].reshape(count * capacity, width)
    gate = gates[:, here, :][:, :, :1].reshape(count * capacity, 1)
    act, _, gate_pre_grads, up_pre_grads = hidden_units(
        rows, grads, gate, gate_w[0], up_w[0], down_w[0]
    )
    act = (act.astype(f32) * gate).astype(bf16)
    terms = (dot_tn(rows, gate_pre_grads), dot_tn(rows, up_pre_grads), dot_tn(act, grads))
    for i, (out, term) in enumerate(zip((gate_out, up_out, down_out), terms)):
        out[0] = term + sums[i][0] if more else term


def weight_path(owner, pairs, weights, after, sums, sizes):
    length, owners, local, capacity = sizes
    width, hidden_wide = weights[0].shape[1:]
    count, slots = sum(rows.shape[0] for rows, _ in pairs), local * capacity
    flops = 2 * count * slots * width * (6 * hidden_wide + 2 * length)
    args = [a for pair in pairs for a in pair]
    shapes = [weights[0].shape, weights[1].shape, weights[2].shape]
    more = sums is not None
    first = 1 + len(args) + 3 + 1
    return pl.pallas_call(
        functools.partial(weight_kernel, blocks=len(pairs), sizes=sizes, more=more),
        grid_spec=pltpu.PrefetchScalarGridSpec(
            num_scalar_prefetch=1,
            grid=(local,),
            in_specs=[whole(a.shape) for a in args]
            + [per_expert(s[1:]) for s in shapes]
            + [pl.BlockSpec(memory_space=pl.ANY)]
            + ([per_expert(s[1:]) for s in shapes] if more else []),
            out_specs=[per_expert(s[1:]) for s in shapes] + [whole((8, 128))],
            scratch_shapes=[
                pltpu.VMEM((count, slots, length), bf16),
                pltpu.VMEM((count, slots, 128), f32),
                pltpu.VMEM((count, slots, width), bf16),
                pltpu.VMEM((count, slots, width), bf16),
            ],
        ),
        out_shape=[jax.ShapeDtypeStruct(s, f32) for s in shapes]
        + [jax.ShapeDtypeStruct((8, 128), f32)],
        input_output_aliases={first + i: i for i in range(3)} if more else {},
        compiler_params=pltpu.CompilerParams(vmem_limit_bytes=62 * 2**20),
        cost_estimate=pl.CostEstimate(flops=flops, bytes_accessed=60 * 2**20, transcendentals=0),
        name="experts_weights",
    )(owner, *args, *weights, after, *(sums or ()))


class Net:
    def __init__(self, owners, shards):
        self.owners, self.shards, self.levels = owners, shards, owners // 2
        self.square = shards == 4
        place = lax.axis_index("expert")
        self.owner, self.core, self.level = place, place % 2, place // 2
        self.shard = lax.axis_index("shard")

    def swap(self, x):
        return lax.ppermute(x, "expert", [(i, i ^ 1) for i in range(self.owners)])

    def lift(self, x, by):
        return lax.ppermute(
            x, "expert", [(i, (i + 2 * by) % self.owners) for i in range(self.owners)]
        )

    def flip(self, x, bits):
        return lax.ppermute(x, "shard", [(i, i ^ bits) for i in range(self.shards)])

    def over_expert(self, x):
        mine = jnp.stack([x] + [self.lift(x, k) for k in range(1, self.levels)])
        return mine, self.swap(mine)

    def home(self, mine, other):
        both = mine + self.swap(other.astype(bf16)).astype(f32)
        total = both[0]
        for k in range(1, self.levels):
            total = total + self.lift(both[k].astype(bf16), self.levels - k).astype(f32)
        return total

    def over_square(self, x):
        half = x.shape[0] // 2
        one, two = self.flip(x, 1), self.flip(x, 2)
        return (one,), (two,), (self.flip(two[:half], 1), self.flip(one[half:], 2))

    def gather_rows(self, x):
        if not self.square:
            return lax.all_gather(x, "shard", axis=0, tiled=True)
        rows = x.shape[0] // 2
        half = lax.dynamic_slice_in_dim(x, self.core * rows, rows, 0)
        (one,), (two,), three = self.over_square(half)
        rel = jnp.stack([half, one, two, jnp.concatenate(three)])
        other = self.swap(rel)
        low = jnp.where(self.core == 0, rel, other)
        high = jnp.where(self.core == 0, other, rel)
        full = jnp.stack([low, high], 1)
        full = full[jnp.arange(self.shards) ^ self.shard]
        return full.reshape((self.shards * x.shape[0],) + x.shape[1:])

    def sum_rows(self, x):
        if not self.square:
            part = lax.psum_scatter(x.astype(bf16), "shard", scatter_dimension=0, tiled=True)
            return lax.psum(part, "expert").astype(f32)
        rows = x.shape[0] // self.shards // 2
        wide = x.shape[1]
        blocks = x.reshape(self.shards, 2, rows, wide)[jnp.arange(self.shards) ^ self.shard]
        mine = lax.dynamic_index_in_dim(blocks, self.core, 1, False)
        other = lax.dynamic_index_in_dim(blocks, 1 - self.core, 1, False)
        chip = mine + self.swap(other.astype(bf16)).astype(f32)
        cut = wide // 256 * 128
        ends = []
        for part, first, second in ((chip[..., :cut], 1, 2), (chip[..., cut:], 2, 1)):
            near, far = self.flip(part[first].astype(bf16), first), self.flip(part[3].astype(bf16), first)
            last = self.flip((part[second] + far.astype(f32)).astype(bf16), second)
            ends.append(part[0] + near.astype(f32) + last.astype(f32))
        own = jnp.concatenate(ends, 1)
        levels = self.levels
        parts = own.reshape(levels, rows // levels, wide)
        part_of = lambda at: lax.dynamic_index_in_dim(parts, at % levels, 0, False)
        total = part_of(self.level)
        for k in range(1, levels):
            total = total + self.lift(part_of(self.level + k).astype(bf16), k).astype(f32)
        total = total.astype(bf16)
        found = jnp.stack([total] + [self.lift(total, k) for k in range(1, levels)])
        found = found[(self.level - jnp.arange(levels)) % levels].reshape(rows, wide)
        twin = self.swap(found)
        low = jnp.where(self.core == 0, found, twin)
        high = jnp.where(self.core == 0, twin, found)
        return jnp.concatenate([low, high], 0).astype(f32)


def per_device(
    hidden_in,
    segment_ids,
    pad_mask,
    expert_choice,
    slot_rank,
    attn_gain,
    query_weight,
    key_weight,
    value_weight,
    output_weight,
    moe_gain,
    router_weight,
    gate_weight,
    up_weight,
    down_weight,
    out_grad,
):
    owners, shards = lax.axis_size("expert"), lax.axis_size("shard")
    net = Net(owners, shards)
    hidden = hidden_in[0].astype(f32)
    length, width = hidden.shape
    segments = segment_ids[0]
    live_int = pad_mask[0]
    live = live_int.astype(f32)
    choices = expert_choice[0]
    ranks = slot_rank[0]
    top_count = choices.shape[1]
    local_experts = gate_weight.shape[0]
    experts_all = owners * local_experts
    capacity = length * top_count // experts_all
    slots = local_experts * capacity
    kv_groups = HEADS // KV_HEADS
    score_scale = HEAD ** (-0.5)
    heads_wide, kv_wide = HEADS * HEAD, KV_HEADS * HEAD

    ids = jnp.arange(experts_all, dtype=jnp.int32)
    picked = jnp.any(choices.T[:, None, :] == ids[None, :, None], 0)
    active = (picked & (live_int > 0)[None, :]).astype(bf16)
    earlier = (ranks[:, None] < ranks[None, :]).astype(bf16)
    places = mm("et,tu->eu", active, earlier)
    kept = picked & (live_int > 0)[None, :] & (places < capacity)
    codes = jnp.where(kept, places, -1.0).astype(bf16)

    tail_wide = local_experts * length

    def tail_row(values):
        return jnp.pad(values.reshape(-1, tail_wide), ((0, 0), (0, width - tail_wide)))

    def with_tail(rows, first, second):
        return jnp.concatenate([rows, tail_row(first), tail_row(second)], 0)

    grad_two = (live[:, None] * out_grad[0].astype(f32)).astype(bf16)
    grad_block = with_tail(grad_two, codes, jnp.zeros_like(codes))
    grad_mine, grad_other = net.over_expert(grad_block)

    misc = jnp.concatenate(
        [router_weight, attn_gain[:, None], moe_gain[:, None]], 1
    )
    misc = jnp.pad(misc, ((0, 0), (0, 128 - misc.shape[1])))
    full = net.gather_rows(
        jnp.concatenate([query_weight, key_weight, value_weight, output_weight, misc], 1)
    )
    cuts = [heads_wide, heads_wide + kv_wide, heads_wide + 2 * kv_wide]
    query_full, key_full, value_full, output_full, misc = jnp.split(
        full, cuts + [cuts[-1] + width], 1
    )
    router_full = misc[:, :experts_all]
    gain_one = misc[:, experts_all].astype(f32)
    gain_two = misc[:, experts_all + 1].astype(f32)

    inv_one = lax.rsqrt(jnp.mean(hidden * hidden, -1, keepdims=True) + eps)
    normed_one = hidden * inv_one
    attn_in = (normed_one * gain_one).astype(bf16)
    cosine, sine_table = rope_tables(segments, HEAD)
    query_raw = jnp.dot(attn_in, query_full, preferred_element_type=f32)
    query_rot = (
        rotate(query_raw.reshape(length, HEADS, HEAD), cosine, sine_table)
        .astype(bf16)
        .reshape(length, KV_HEADS, kv_groups, HEAD)
    )
    key_raw = jnp.dot(attn_in, key_full, preferred_element_type=f32)
    key_rot = rotate(key_raw.reshape(length, KV_HEADS, HEAD), cosine, sine_table).astype(bf16)
    value_rows = (
        jnp.dot(attn_in, value_full, preferred_element_type=f32)
        .astype(bf16)
        .reshape(length, KV_HEADS, HEAD)
    )
    allowed = allowed_mask(segments, live_int)

    def score_block():
        raw_scores = mm("qgrd,kgd->grqk", query_rot, key_rot) * score_scale
        return jnp.where(allowed[None, None], raw_scores, masked)

    scores = score_block()
    top_score = jnp.max(scores, -1, keepdims=True)
    log_total = top_score + jnp.log(jnp.sum(jnp.exp(scores - top_score), -1, keepdims=True))
    probs = jnp.exp(scores - log_total)
    mixed = mm("grqk,kgd->qgrd", probs.astype(bf16), value_rows)
    attn_out = mixed.astype(bf16).reshape(length, heads_wide)
    resid_one = hidden + jnp.dot(attn_out, output_full, preferred_element_type=f32)
    inv_two = lax.rsqrt(jnp.mean(resid_one * resid_one, -1, keepdims=True) + eps)
    normed_two = resid_one * inv_two
    moe_in = (normed_two * gain_two).astype(bf16)
    logits = mm("de,td->et", router_full, moe_in)
    top_logit = jnp.max(jnp.where(picked, logits, masked), 0, keepdims=True)
    powers = jnp.where(picked, jnp.exp(jnp.minimum(logits - top_logit, 0.0)), 0.0)
    gates = powers / jnp.sum(powers, 0, keepdims=True)
    gates_kept = jnp.where(kept, gates, 0.0)
    gates_high = gates_kept.astype(bf16)
    gates_low = (gates_kept - gates_high.astype(f32)).astype(bf16)
    row_block = with_tail(moe_in, gates_high, gates_low)
    rows_mine, rows_other = net.over_expert(row_block)

    sizes = (length, owners, local_experts, capacity)
    weights = (gate_weight, up_weight, down_weight)
    owner = net.owner.reshape(1).astype(jnp.int32)
    levels, step = net.levels, min(net.levels, 4)
    found, terms = [], None
    for low in range(0, levels, step):
        cut = slice(low, low + step)
        rows, grads = (rows_mine[cut], rows_other[cut]), (grad_mine[cut], grad_other[cut])
        found.append(data_path(owner, rows, grads, weights, sizes))
    token = found[-1][-1]
    branch_mine, branch_other, back_mine, back_other = (
        found[0][i] if step == levels else jnp.concatenate([f[i] for f in found]) for i in range(4)
    )
    for low in range(0, levels, step):
        cut = slice(low, low + step)
        pairs = [(rows_mine[cut], grad_mine[cut]), (rows_other[cut], grad_other[cut])]
        *terms, token = weight_path(owner, pairs, weights, token, terms, sizes)
    back = net.home(back_mine, back_other)
    branch = net.home(branch_mine, branch_other)
    if net.square:
        for rows, grads in zip(net.over_square(rows_mine), net.over_square(grad_mine)):
            pairs = list(zip(rows, grads))
            pairs += [(net.swap(a), net.swap(b)) for a, b in pairs]
            *terms, token = weight_path(owner, pairs, weights, token, terms, sizes)
    else:
        terms = tuple(lax.psum(a.astype(bf16), "shard").astype(f32) for a in terms)

    block_out = (live[:, None] * (resid_one + branch)).astype(bf16)
    gate_grads = back[length : length + owners] + back[length + owners :]
    gate_grads = gate_grads[:, :tail_wide].reshape(experts_all, length)
    gate_inner = jnp.sum(gates * gate_grads, 0, keepdims=True)
    logit_grads = (gates * (gate_grads - gate_inner)).astype(bf16)
    router_grad = mm("td,et->de", moe_in, logit_grads)
    moe_in_grads = back[:length] + mm("et,de->td", logit_grads, router_full)
    gain_two_grad = jnp.sum(moe_in_grads * normed_two, 0)
    resid_grad = grad_two.astype(f32) + norm_back(moe_in_grads * gain_two, normed_two, inv_two)
    branch_grad = resid_grad.astype(bf16)
    output_grad_w = mm("lh,ld->hd", attn_out, branch_grad)
    mixed_grad = mm("ld,hd->lh", branch_grad, output_full)
    mixed_grad = mixed_grad.astype(bf16).reshape(length, KV_HEADS, kv_groups, HEAD)
    probs_again = jnp.exp(score_block() - log_total)
    prob_grads = mm("qgrd,kgd->grqk", mixed_grad, value_rows)
    value_grad = mm("grqk,qgrd->kgd", probs_again.astype(bf16), mixed_grad)
    value_grad = value_grad.astype(bf16).reshape(length, kv_wide)
    score_grads = (
        probs_again * (prob_grads - jnp.sum(probs_again * prob_grads, -1, keepdims=True))
    ).astype(bf16)
    query_rot_grad = mm("grqk,kgd->qgrd", score_grads, key_rot) * score_scale
    key_rot_grad = mm("grqk,qgrd->kgd", score_grads, query_rot) * score_scale
    query_grad = (
        unrotate(query_rot_grad.reshape(length, HEADS, HEAD), cosine, sine_table)
        .astype(bf16)
        .reshape(length, heads_wide)
    )
    key_grad = unrotate(key_rot_grad, cosine, sine_table).astype(bf16).reshape(length, kv_wide)
    query_grad_w = mm("ld,lh->dh", attn_in, query_grad)
    key_grad_w = mm("ld,lh->dh", attn_in, key_grad)
    value_grad_w = mm("ld,lh->dh", attn_in, value_grad)
    attn_in_grads = mm("lh,dh->ld", query_grad, query_full)
    attn_in_grads = attn_in_grads + mm("lh,dh->ld", key_grad, key_full)
    attn_in_grads = attn_in_grads + mm("lh,dh->ld", value_grad, value_full)
    gain_one_grad = jnp.sum(attn_in_grads * normed_one, 0)
    hidden_grad = resid_grad + norm_back(attn_in_grads * gain_one, normed_one, inv_one)
    misc_grad = jnp.concatenate([router_grad, gain_one_grad[:, None], gain_two_grad[:, None]], 1)
    misc_grad = jnp.pad(misc_grad, ((0, 0), (0, 128 - misc_grad.shape[1])))
    sums = net.sum_rows(
        jnp.concatenate([query_grad_w, key_grad_w, value_grad_w, output_grad_w, misc_grad], 1)
    )
    sum_query, sum_key, sum_value, sum_output, sum_misc = jnp.split(
        sums, cuts + [cuts[-1] + width], 1
    )
    return (
        block_out[None],
        hidden_grad.astype(bf16)[None],
        sum_misc[:, experts_all],
        sum_query,
        sum_key,
        sum_value,
        sum_output,
        sum_misc[:, experts_all + 1],
        sum_misc[:, :experts_all],
        terms[0],
        terms[1],
        terms[2],
    )


def solution(mesh):
    tokens = ("expert", "shard")
    in_specs = (
        P(tokens, None, None),
        P(tokens, None),
        P(tokens, None),
        P(tokens, None, None),
        P(tokens, None),
        P("shard"),
        P("shard", None),
        P("shard", None),
        P("shard", None),
        P("shard", None),
        P("shard"),
        P("shard", None),
        P("expert", None, None),
        P("expert", None, None),
        P("expert", None, None),
        P(tokens, None, None),
    )
    out_specs = (
        P(tokens, None, None),
        P(tokens, None, None),
        P("shard"),
        P("shard", None),
        P("shard", None),
        P("shard", None),
        P("shard", None),
        P("shard"),
        P("shard", None),
        P("expert", None, None),
        P("expert", None, None),
        P("expert", None, None),
    )
    return jax.shard_map(
        per_device, mesh=mesh, in_specs=in_specs, out_specs=out_specs, check_vma=False
    )
```
